32 devices in a mesh: dp: 4 (over z), ctx: 2 (over x), head: 4 (over y, core).
Axes of the slice: x: 2, y: 2, z: 4, core: 2. Of those that a mesh axis runs over, the one named last changes fastest.
Arguments:
- block_in: bfloat16 [4096, 640], P(('dp', 'ctx', 'head')), may hold values from -6 to 6
- cotangent: bfloat16 [4096, 640], P(('dp', 'ctx', 'head')), may hold values from -6 to 6
- positions: int32 [4096], P(('dp', 'ctx')), may hold values from 0 to 1023, as said below
- norm_gains: float32 [4, 640], replicated, may hold values from 0.5 to 1.5
- qk_gains: float32 [2, 256], replicated, may hold values from 0.5 to 1.5
- w_query: bfloat16 [640, 1024], P(None, ('dp', 'ctx', 'head')), may hold values from -0.25 to 0.25
- w_key: bfloat16 [640, 256], P(None, ('dp', 'ctx', 'head')), may hold values from -0.25 to 0.25
- w_value: bfloat16 [640, 256], P(None, ('dp', 'ctx', 'head')), may hold values from -0.25 to 0.25
- w_out: bfloat16 [1024, 640], P(('dp', 'ctx', 'head')), may hold values from -0.75 to 0.75
- w_gate: bfloat16 [640, 2048], P(None, ('dp', 'ctx', 'head')), may hold values from -0.25 to 0.25
- w_up: bfloat16 [640, 2048], P(None, ('dp', 'ctx', 'head')), may hold values from -0.25 to 0.25
- w_down: bfloat16 [2048, 640], P(('dp', 'ctx', 'head')), may hold values from -0.125 to 0.125
Outputs:
- block_out: bfloat16 [4096, 640], P(('dp', 'ctx', 'head'))
- d_block_in: bfloat16 [4096, 640], P(('dp', 'ctx', 'head'))
- grad_norm_gains: float32 [4, 640], replicated
- grad_qk_gains: float32 [2, 256], replicated
- grad_query: float32 [640, 1024], P(None, ('dp', 'ctx', 'head'))
- grad_key: float32 [640, 256], P(None, ('dp', 'ctx', 'head'))
- grad_value: float32 [640, 256], P(None, ('dp', 'ctx', 'head'))
- grad_out: float32 [1024, 640], P(('dp', 'ctx', 'head'))
- grad_gate: float32 [640, 2048], P(None, ('dp', 'ctx', 'head'))
- grad_up: float32 [640, 2048], P(None, ('dp', 'ctx', 'head'))
- grad_down: float32 [2048, 640], P(('dp', 'ctx', 'head'))
The draws below stay inside these ranges and needn't reach their ends.
Inputs may be any that keep to these rules, and one draw needn't show every extreme that they name: Each sequence of 1024 tokens holds one or two documents: positions count from 0 at the sequence's first token and restart from 0 at most once.
All inputs are finite; a program needn't handle non-finite values.
Results may differ from the reference program's by a relative error of at most 0.019.
Values may be sent and summed in bfloat16 or wider, within the bound.
A program may use at most 128 MiB of HBM per device.

```python
import math
import jax
import jax.numpy as jnp
from jax import lax

D = 640
HEADS = 4
HEAD_DIM = 256
FF = 2048
LENGTH = 1024
TOKENS = 4096
KEY_BLOCK = 512


def draw_positions(key, part):
    seq_count = TOKENS // LENGTH
    cut_points = jax.random.randint(key, (seq_count,), LENGTH // 4, 3 * LENGTH // 4 + 1)
    cut_points = jnp.where(jnp.arange(seq_count) == 0, LENGTH, cut_points).astype(jnp.int32)
    ladder = jnp.arange(LENGTH, dtype=jnp.int32)
    placed = jnp.where(ladder[None, :] < cut_points[:, None], ladder[None, :], ladder[None, :] - cut_points[:, None])
    return placed.reshape(TOKENS).astype(jnp.int32)


def levels(own_key, extent, shards, low, largest):
    factor_of = 1.0
    for axis_at, parts in shards:
        draws = jax.random.uniform(jax.random.fold_in(jax.random.fold_in(own_key, 6), axis_at), (parts,), jnp.float32, low / len(shards), largest / len(shards))
        factor_of = factor_of * jnp.repeat(jnp.exp(draws), extent[axis_at] // parts).reshape((-1,) + (1,) * (len(extent) - 1 - axis_at))
    return factor_of


def gaussian(stream_key, shape, scale, limit, cuts=(), held_as=jnp.bfloat16):
    result = scale * jax.random.normal(stream_key, shape, jnp.float32)
    if cuts:
        result = result * levels(stream_key, shape, cuts, -0.22, 0.18)
    return jnp.clip(result, -limit, limit).astype(held_as)


def setup_inputs(seed: int = 0) -> dict:
    keys = jax.random.split(jax.random.key(seed), 13)
    return {
        "block_in": gaussian(keys[0], (TOKENS, D), 1.0, 6.0, ((0, 32),)),
        "cotangent": gaussian(keys[1], (TOKENS, D), 1.0, 6.0, ((0, 32),)),
        "positions": draw_positions(jax.random.fold_in(keys[12], 71), 0),
        "norm_gains": jnp.clip(1.0 + 0.1 * jax.random.normal(keys[3], (4, D), jnp.float32), 0.5, 1.5),
        "qk_gains": jnp.clip(1.0 + 0.1 * jax.random.normal(keys[4], (2, HEAD_DIM), jnp.float32), 0.5, 1.5),
        "w_query": gaussian(keys[5], (D, HEADS * HEAD_DIM), D ** -0.5, 0.25, ((1, 32),)),
        "w_key": gaussian(keys[6], (D, HEAD_DIM), D ** -0.5, 0.25, ((1, 32),)),
        "w_value": gaussian(keys[7], (D, HEAD_DIM), D ** -0.5, 0.25, ((1, 32),)),
        "w_out": gaussian(keys[8], (HEADS * HEAD_DIM, D), (HEADS * HEAD_DIM // 16) ** -0.5, 0.75, ((0, 32),)),
        "w_gate": gaussian(keys[9], (D, FF), D ** -0.5, 0.25, ((1, 32),)),
        "w_up": gaussian(keys[10], (D, FF), D ** -0.5, 0.25, ((1, 32),)),
        "w_down": gaussian(keys[11], (FF, D), FF ** -0.5, 0.125, ((0, 32),)),
    }


epsilon = 1e-06
rope_base = 1000000.0
score_scale = 0.0625
negative_fill = -1e+30

def norm_rows(values, gain_vec):
    inverse = lax.rsqrt(lax.optimization_barrier(jnp.mean(values * values, axis=-1, keepdims=True)) + epsilon)
    return (values * inverse * gain_vec, inverse)

def norm_back(values, inverse, gain_vec, upstream):
    scaled = upstream * gain_vec
    inner_mean = lax.optimization_barrier(jnp.mean(scaled * values, axis=-1, keepdims=True))
    return (inverse * scaled - values * (inverse * inverse * inverse) * inner_mean, upstream * values * inverse)

def rope_angles(positions, full_width):
    ladder = jnp.arange(full_width // 2, dtype=jnp.float32)
    frequency = jnp.exp(ladder * (-2.0 / full_width) * math.log(rope_base))
    angles = positions.astype(jnp.float32)[:, None] * frequency[None, :]
    return (jnp.cos(angles), jnp.sin(angles))

def rotate(values, cosine, sine_part):
    middle = values.shape[-1] // 2
    first_half = values[..., :middle]
    second = values[..., middle:]
    return jnp.concatenate([first_half * cosine - second * sine_part, second * cosine + first_half * sine_part], axis=-1)

def gelu_product(gate_pre, up_pre):
    return jax.nn.gelu(gate_pre, approximate=True) * up_pre

def rounded(values):
    return lax.optimization_barrier(values.astype(jnp.bfloat16)).astype(jnp.float32)

def masked_scores(query_part, keys_wide, query_index, query_pos):
    scores = jnp.einsum('hqd,kd->hqk', query_part, keys_wide)
    key_index = jnp.arange(keys_wide.shape[0], dtype=jnp.int32)
    lowest_key = query_index - query_pos
    visible = (key_index[None, :] <= query_index[:, None]) & (key_index[None, :] >= lowest_key[:, None])
    return jnp.where(visible[None], scores, negative_fill)

def reference(block_in, cotangent, positions, norm_gains, qk_gains, w_query, w_key, w_value, w_out, w_gate, w_up, w_down):
    seq_count = TOKENS // LENGTH
    block_total = LENGTH // KEY_BLOCK

    def one_sequence(totals, seq_items):
        seq_in, seq_cot, seq_pos = seq_items
        input_wide = seq_in.astype(jnp.float32)
        attn_norm, inverse_in = norm_rows(input_wide, norm_gains[0])
        attn_in = attn_norm.astype(jnp.bfloat16)
        query_raw = jnp.dot(attn_in, w_query, preferred_element_type=jnp.float32).reshape(LENGTH, HEADS, HEAD_DIM)
        key_raw = jnp.dot(attn_in, w_key, preferred_element_type=jnp.float32)
        value_rows = jnp.dot(attn_in, w_value, preferred_element_type=jnp.float32).astype(jnp.bfloat16)
        query_normed, inverse_query = norm_rows(query_raw, qk_gains[0])
        key_normed, inverse_key = norm_rows(key_raw, qk_gains[1])
        cosine, sine_part = rope_angles(seq_pos, HEAD_DIM)
        rot_query = (rotate(query_normed, cosine[:, None], sine_part[:, None]) * score_scale).astype(jnp.bfloat16)
        rot_key = rotate(key_normed, cosine, sine_part).astype(jnp.bfloat16)
        head_query = jnp.transpose(rot_query, (1, 0, 2)).astype(jnp.float32)
        keys_wide = rot_key.astype(jnp.float32)
        values_wide = value_rows.astype(jnp.float32)
        all_index = jnp.arange(LENGTH, dtype=jnp.int32)
        total_blocks = []
        exact_blocks = []
        for block_index in range(block_total):
            row_start = block_index * KEY_BLOCK
            finish = row_start + KEY_BLOCK
            scores = masked_scores(head_query[:, row_start:finish], keys_wide[:finish], all_index[row_start:finish], seq_pos[row_start:finish])
            row_top = lax.optimization_barrier(jnp.max(scores, axis=-1, keepdims=True))
            log_total = row_top + jnp.log(lax.optimization_barrier(jnp.sum(jnp.exp(scores - row_top), axis=-1, keepdims=True)))
            prob_rows = rounded(jnp.exp(scores - log_total))
            total_blocks.append(log_total)
            exact_blocks.append(jnp.einsum('hqk,kd->hqd', prob_rows, values_wide[:finish]))
        attn_exact = jnp.concatenate(exact_blocks, axis=1)
        attn_out = jnp.transpose(attn_exact, (1, 0, 2)).astype(jnp.bfloat16).reshape(LENGTH, HEADS * HEAD_DIM)
        branch = jnp.dot(attn_out, w_out, preferred_element_type=jnp.float32)
        branch_normed, inverse_branch = norm_rows(branch, norm_gains[1])
        middle = input_wide + branch_normed
        mlp_norm, inverse_mid = norm_rows(middle, norm_gains[2])
        mlp_in = mlp_norm.astype(jnp.bfloat16)
        gate_pre = jnp.dot(mlp_in, w_gate, preferred_element_type=jnp.float32)
        up_pre = jnp.dot(mlp_in, w_up, preferred_element_type=jnp.float32)
        hidden = gelu_product(gate_pre, up_pre).astype(jnp.bfloat16)
        down_raw = jnp.dot(hidden, w_down, preferred_element_type=jnp.float32)
        down_normed, inverse_down = norm_rows(down_raw, norm_gains[3])
        block_out = (middle + down_normed).astype(jnp.bfloat16)
        cot_wide = seq_cot.astype(jnp.float32)
        grad_down_raw, gain_three = norm_back(down_raw, inverse_down, norm_gains[3], cot_wide)
        grad_down_in = grad_down_raw.astype(jnp.bfloat16)
        grad_down = jnp.dot(hidden.T, grad_down_in, preferred_element_type=jnp.float32)
        grad_hidden = jnp.dot(grad_down_in, w_down.T, preferred_element_type=jnp.float32)
        _, gelu_pull = jax.vjp(gelu_product, gate_pre, up_pre)
        grad_gate_raw, grad_up_raw = gelu_pull(grad_hidden)
        grad_gate_in = grad_gate_raw.astype(jnp.bfloat16)
        grad_up_in = grad_up_raw.astype(jnp.bfloat16)
        grad_gate = jnp.dot(mlp_in.T, grad_gate_in, preferred_element_type=jnp.float32)
        grad_up = jnp.dot(mlp_in.T, grad_up_in, preferred_element_type=jnp.float32)
        grad_mlp_in = jnp.dot(grad_gate_in, w_gate.T, preferred_element_type=jnp.float32) + jnp.dot(grad_up_in, w_up.T, preferred_element_type=jnp.float32)
        grad_mid_part, gain_two = norm_back(middle, inverse_mid, norm_gains[2], grad_mlp_in)
        grad_middle = cot_wide + grad_mid_part
        grad_branch_raw, gain_one = norm_back(branch, inverse_branch, norm_gains[1], grad_middle)
        grad_branch = grad_branch_raw.astype(jnp.bfloat16)
        grad_out = jnp.dot(attn_out.T, grad_branch, preferred_element_type=jnp.float32)
        grad_attn = jnp.dot(grad_branch, w_out.T, preferred_element_type=jnp.float32).astype(jnp.bfloat16)
        head_grad = jnp.transpose(grad_attn.reshape(LENGTH, HEADS, HEAD_DIM), (1, 0, 2)).astype(jnp.float32)
        key_sums = jnp.zeros((LENGTH, HEAD_DIM), jnp.float32)
        value_sums = jnp.zeros((LENGTH, HEAD_DIM), jnp.float32)
        query_blocks = []
        for block_index in range(block_total):
            row_start = block_index * KEY_BLOCK
            finish = row_start + KEY_BLOCK
            query_part = head_query[:, row_start:finish]
            scores = masked_scores(query_part, keys_wide[:finish], all_index[row_start:finish], seq_pos[row_start:finish])
            probs_wide = jnp.exp(scores - total_blocks[block_index])
            grad_part = head_grad[:, row_start:finish]
            row_delta = lax.optimization_barrier(jnp.sum(grad_part * exact_blocks[block_index], axis=-1, keepdims=True))
            value_sums = value_sums.at[:finish].add(jnp.einsum('hqk,hqd->kd', rounded(probs_wide), grad_part))
            grad_probs = jnp.einsum('hqd,kd->hqk', grad_part, values_wide[:finish])
            grad_scores = rounded(probs_wide * (grad_probs - row_delta))
            query_blocks.append(jnp.einsum('hqk,kd->hqd', grad_scores, keys_wide[:finish]))
            key_sums = key_sums.at[:finish].add(jnp.einsum('hqk,hqd->kd', grad_scores, query_part))
        grad_rot_query = jnp.transpose(jnp.concatenate(query_blocks, axis=1), (1, 0, 2))
        query_back = rotate(grad_rot_query * score_scale, cosine[:, None], -sine_part[:, None])
        grad_query_raw, gain_query = norm_back(query_raw, inverse_query, qk_gains[0], query_back)
        key_back = rotate(key_sums, cosine, -sine_part)
        grad_key_raw, gain_key = norm_back(key_raw, inverse_key, qk_gains[1], key_back)
        grad_query_in = grad_query_raw.reshape(LENGTH, HEADS * HEAD_DIM).astype(jnp.bfloat16)
        grad_key_in = grad_key_raw.astype(jnp.bfloat16)
        grad_value_in = value_sums.astype(jnp.bfloat16)
        grad_query = jnp.dot(attn_in.T, grad_query_in, preferred_element_type=jnp.float32)
        grad_key = jnp.dot(attn_in.T, grad_key_in, preferred_element_type=jnp.float32)
        grad_value = jnp.dot(attn_in.T, grad_value_in, preferred_element_type=jnp.float32)
        grad_attn_in = jnp.dot(grad_query_in, w_query.T, preferred_element_type=jnp.float32)
        grad_attn_in = grad_attn_in + jnp.dot(grad_key_in, w_key.T, preferred_element_type=jnp.float32)
        grad_attn_in = grad_attn_in + jnp.dot(grad_value_in, w_value.T, preferred_element_type=jnp.float32)
        grad_in_part, gain_zero = norm_back(input_wide, inverse_in, norm_gains[0], grad_attn_in)
        d_block_in = (grad_middle + grad_in_part).astype(jnp.bfloat16)
        gain_terms = jnp.stack([lax.optimization_barrier(jnp.sum(gain_zero, axis=0)), lax.optimization_barrier(jnp.sum(gain_one, axis=0)), lax.optimization_barrier(jnp.sum(gain_two, axis=0)), lax.optimization_barrier(jnp.sum(gain_three, axis=0))])
        qk_terms = jnp.stack([lax.optimization_barrier(jnp.sum(gain_query, axis=(0, 1))), lax.optimization_barrier(jnp.sum(gain_key, axis=0))])
        fresh = (gain_terms, qk_terms, grad_query, grad_key, grad_value, grad_out, grad_gate, grad_up, grad_down)
        return (jax.tree.map(lambda older, newer: older + newer, totals, fresh), (block_out, d_block_in))
    starting = (jnp.zeros((4, D), jnp.float32), jnp.zeros((2, HEAD_DIM), jnp.float32), jnp.zeros((D, HEADS * HEAD_DIM), jnp.float32), jnp.zeros((D, HEAD_DIM), jnp.float32), jnp.zeros((D, HEAD_DIM), jnp.float32), jnp.zeros((HEADS * HEAD_DIM, D), jnp.float32), jnp.zeros((D, FF), jnp.float32), jnp.zeros((D, FF), jnp.float32), jnp.zeros((FF, D), jnp.float32))
    totals, (outs_seq, grads_seq) = lax.scan(one_sequence, starting, (block_in.reshape(seq_count, LENGTH, D), cotangent.reshape(seq_count, LENGTH, D), positions.reshape(seq_count, LENGTH)))
    return (outs_seq.reshape(TOKENS, D), grads_seq.reshape(TOKENS, D), totals[0], totals[1], totals[2], totals[3], totals[4], totals[5], totals[6], totals[7], totals[8])
```

```python
import math

import jax
import jax.numpy as jnp
from jax import lax
from jax.experimental import pallas as pl
from jax.experimental.pallas import tpu as pltpu
from jax.sharding import PartitionSpec as P

epsilon = 1e-06
rope_base = 1000000.0
score_scale = 0.0625
negative_fill = -1e30


def norm_rows(values, gain_vec):
    inverse = lax.rsqrt(jnp.mean(values * values, axis=-1, keepdims=True) + epsilon)
    return (values * inverse * gain_vec, inverse)


def norm_back(values, inverse, gain_vec, upstream):
    scaled = upstream * gain_vec
    inner_mean = jnp.mean(scaled * values, axis=-1, keepdims=True)
    return (
        inverse * scaled - values * (inverse * inverse * inverse) * inner_mean,
        upstream * values * inverse,
    )


def rope_angles(positions, full_width):
    ladder = jnp.arange(full_width // 2, dtype=jnp.float32)
    frequency = jnp.exp(ladder * (-2.0 / full_width) * math.log(rope_base))
    angles = positions.astype(jnp.float32)[:, None] * frequency[None, :]
    return (jnp.cos(angles), jnp.sin(angles))


def rotate(values, cosine, sine_part):
    middle = values.shape[-1] // 2
    first_half = values[..., :middle]
    second = values[..., middle:]
    return jnp.concatenate(
        [first_half * cosine - second * sine_part, second * cosine + first_half * sine_part],
        axis=-1,
    )


def gelu_product(gate_pre, up_pre):
    return jax.nn.gelu(gate_pre, approximate=True) * up_pre


every_axis = ("dp", "ctx", "head")
sequence_axes = ("ctx", "head")
weight_axes = ("dp", "ctx")


def place_in(axes):
    place = 0
    for name in axes:
        place = place * lax.axis_size(name) + lax.axis_index(name)
    return place


def coordinates(axes, place):
    found = {}
    for name in reversed(axes):
        size = lax.axis_size(name)
        found[name] = lax.rem(place, size)
        place = place // size
    return found


def each_peer(count, step):
    if count <= 8:
        for offset in range(1, count):
            step(offset)
    else:

        def looped(offset, carry):
            step(offset)
            return carry

        lax.fori_loop(1, count, looped, 0)


def exchange_kernel(kinds, greet, counts, *refs):
    total = len(kinds)
    sources, targets, sems = refs[:total], refs[total : 2 * total], refs[2 * total :]
    barrier = pltpu.get_barrier_semaphore()
    waits = 0
    for axes, count in greet:
        me = place_in(axes)

        def greet_peer(offset, axes=axes, count=count, me=me):
            pl.semaphore_signal(
                barrier,
                inc=1,
                device_id=coordinates(axes, lax.rem(me + offset, count)),
                device_id_type=pl.DeviceIdType.MESH,
            )

        each_peer(count, greet_peer)
        waits += count - 1
    locals_started = []
    for part, (kind, axes) in enumerate(kinds):
        me = place_in(axes)
        source = sources[part].at[me] if kind == "scatter" else sources[part]
        copy = pltpu.make_async_copy(source, targets[part].at[me], sems[3 * part + 2].at[0])
        copy.start()
        locals_started.append(copy)
    pl.semaphore_wait(barrier, waits)

    def descriptor(part, offset, backward):
        kind, axes = kinds[part]
        count = counts[part]
        me = place_in(axes)
        to = lax.rem(me + offset, count)
        origin = lax.rem(me + count - offset, count) if backward else me
        source = sources[part].at[to] if kind == "scatter" else sources[part]
        return pltpu.make_async_remote_copy(
            src_ref=source,
            dst_ref=targets[part].at[origin],
            send_sem=sems[3 * part].at[offset],
            recv_sem=sems[3 * part + 1].at[origin],
            device_id=coordinates(axes, to),
            device_id_type=pl.DeviceIdType.MESH,
        )

    for part in range(total):
        each_peer(counts[part], lambda offset: descriptor(part, offset, False).start())
    for copy in locals_started:
        copy.wait()
    for part in range(total):
        each_peer(counts[part], lambda offset: descriptor(part, offset, True).wait_recv())
    for part in range(total):
        each_peer(counts[part], lambda offset: descriptor(part, offset, False).wait_send())


def exchange(call_id, name, parts, greet_axes=None):
    kinds = tuple((kind, axes) for kind, axes, _ in parts)
    arrays = [array for _, _, array in parts]
    counts = tuple(lax.axis_size(axes) for _, axes in kinds)
    if greet_axes is None:
        greet_axes = kinds[0][1]
    greet = ((greet_axes, lax.axis_size(greet_axes)),)
    shapes = [
        jax.ShapeDtypeStruct(
            array.shape if kind == "scatter" else (count,) + array.shape, array.dtype
        )
        for (kind, _, array), count in zip(parts, counts)
    ]
    scratch = []
    for count in counts:
        scratch += [
            pltpu.SemaphoreType.DMA((count,)),
            pltpu.SemaphoreType.DMA((count,)),
            pltpu.SemaphoreType.DMA((1,)),
        ]
    in_vmem = pl.BlockSpec(memory_space=pltpu.VMEM)
    return pl.pallas_call(
        lambda *refs: exchange_kernel(kinds, greet, counts, *refs),
        out_shape=shapes,
        in_specs=[in_vmem] * len(arrays),
        out_specs=[in_vmem] * len(arrays),
        scratch_shapes=scratch,
        compiler_params=pltpu.CompilerParams(collective_id=call_id, has_side_effects=True),
        name=name,
    )(*arrays)


def rows_dot(left, right, left_dim, right_dim):
    return lax.dot_general(
        left, right, (((left_dim,), (right_dim,)), ((), ())), preferred_element_type=jnp.float32
    )


def add_up(blocks):
    return jnp.sum(blocks.astype(jnp.float32), axis=0)


def local(
    block_in,
    cotangent,
    positions,
    norm_gains,
    qk_gains,
    w_query,
    w_key,
    w_value,
    w_out,
    w_gate,
    w_up,
    w_down,
):
    tok_rows, model_width = block_in.shape
    head_count = lax.axis_size("head")
    head_width = qk_gains.shape[1]
    ctx_slot = lax.axis_index("ctx")
    query_rows = head_count * tok_rows
    group_count = lax.axis_size(weight_axes)
    every_count = lax.axis_size(every_axis)
    length_all = lax.axis_size(sequence_axes) * tok_rows
    query_cols = w_query.shape[1]
    key_cols = w_key.shape[1]
    ff_cols = w_gate.shape[1]
    narrow = jnp.bfloat16

    ff_rows = jnp.concatenate([w_gate.T, w_up.T, w_down], axis=0)
    ff_all = lax.all_gather(ff_rows, weight_axes, axis=0, tiled=False)

    to_heads = [
        (head * group_count + index, index * head_count + head)
        for head in range(head_count)
        for index in range(group_count)
    ]
    to_owners = [(there, here) for here, there in to_heads]
    head_rows = lax.ppermute(
        jnp.concatenate([w_query.T, w_out], axis=0), every_axis, to_heads
    )
    key_value_rows = jnp.concatenate([w_key.T, w_value.T], axis=0)
    block_all, key_value_all, head_all, position_all = exchange(
        1,
        "first_gather",
        [
            ("gather", sequence_axes, block_in),
            ("gather", every_axis, key_value_rows),
            ("gather", weight_axes, head_rows),
            ("gather", ("ctx",), positions.reshape(-1, 128)),
        ],
        every_axis,
    )
    query_weight = head_all[:, :query_cols].reshape(head_width, model_width)
    out_weight = head_all[:, query_cols:].reshape(head_width, model_width)
    key_weight = key_value_all[:, :key_cols].reshape(head_width, model_width)
    value_weight = key_value_all[:, key_cols:].reshape(head_width, model_width)

    input_all = block_all.reshape(length_all, model_width).astype(jnp.float32)
    attn_in_all = norm_rows(input_all, norm_gains[0])[0].astype(narrow)
    first_query = ctx_slot * query_rows
    attn_in = lax.dynamic_slice_in_dim(attn_in_all, first_query, query_rows)
    query_raw = rows_dot(attn_in, query_weight, 1, 1)
    key_raw = rows_dot(attn_in_all, key_weight, 1, 1)
    all_values = rows_dot(attn_in_all, value_weight, 1, 1).astype(narrow)
    query_normed, inverse_query = norm_rows(query_raw, qk_gains[0])
    key_normed, inverse_key = norm_rows(key_raw, qk_gains[1])
    cosine, sine_part = rope_angles(position_all.reshape(length_all), head_width)
    cosine_own = lax.dynamic_slice_in_dim(cosine, first_query, query_rows)
    sine_own = lax.dynamic_slice_in_dim(sine_part, first_query, query_rows)
    head_query = (rotate(query_normed, cosine_own, sine_own) * score_scale).astype(narrow)
    all_keys = rotate(key_normed, cosine, sine_part).astype(narrow)

    query_index = first_query + jnp.arange(query_rows, dtype=jnp.int32)
    lowest_key = query_index - positions
    key_index = jnp.arange(length_all, dtype=jnp.int32)
    visible = (key_index[None, :] <= query_index[:, None]) & (
        key_index[None, :] >= lowest_key[:, None]
    )
    scores = jnp.where(visible, rows_dot(head_query, all_keys, 1, 1), negative_fill)
    top = jnp.max(scores, axis=1, keepdims=True)
    log_total = top + jnp.log(jnp.sum(jnp.exp(scores - top), axis=1, keepdims=True))
    probs_wide = jnp.exp(scores - log_total)
    prob_rows = probs_wide.astype(narrow)
    attn_exact = rows_dot(prob_rows, all_values, 1, 0)
    attn_out = attn_exact.astype(narrow)
    branch_part = rows_dot(attn_out, out_weight, 1, 0).astype(narrow)
    (branch_blocks,) = exchange(
        2,
        "branch_scatter",
        [("scatter", ("head",), branch_part.reshape(head_count, tok_rows, model_width))],
    )
    branch = add_up(branch_blocks)
    input_wide = block_in.astype(jnp.float32)
    inverse_in = norm_rows(input_wide, norm_gains[0])[1]
    branch_normed, inverse_branch = norm_rows(branch, norm_gains[1])
    middle = input_wide + branch_normed
    mlp_norm, inverse_mid = norm_rows(middle, norm_gains[2])
    (mlp_blocks,) = exchange(
        3, "mlp_gather", [("gather", ("head",), mlp_norm.astype(narrow))]
    )
    mlp_in = mlp_blocks.reshape(query_rows, model_width)

    ff_width = group_count * ff_cols
    gate_weight = ff_all[:, :ff_cols].reshape(ff_width, model_width)
    up_weight = ff_all[:, ff_cols : 2 * ff_cols].reshape(ff_width, model_width)
    down_weight = ff_all[:, 2 * ff_cols :].reshape(ff_width, model_width)
    gate_pre = rows_dot(mlp_in, gate_weight, 1, 1)
    up_pre = rows_dot(mlp_in, up_weight, 1, 1)
    hidden = gelu_product(gate_pre, up_pre).astype(narrow)
    down_part = rows_dot(hidden, down_weight, 1, 0).astype(narrow)
    (down_blocks,) = exchange(
        4,
        "down_scatter",
        [("scatter", ("head",), down_part.reshape(head_count, tok_rows, model_width))],
    )
    down_raw = add_up(down_blocks)
    down_normed, inverse_down = norm_rows(down_raw, norm_gains[3])
    block_out = (middle + down_normed).astype(narrow)
    cot_wide = cotangent.astype(jnp.float32)
    grad_down_raw, gain_three = norm_back(down_raw, inverse_down, norm_gains[3], cot_wide)
    (grad_down_blocks,) = exchange(
        5, "grad_down_gather", [("gather", ("head",), grad_down_raw.astype(narrow))]
    )
    grad_down_in = grad_down_blocks.reshape(query_rows, model_width)
    grad_hidden = rows_dot(grad_down_in, down_weight, 1, 1)
    _, gelu_pull = jax.vjp(gelu_product, gate_pre, up_pre)
    grad_gate_raw, grad_up_raw = gelu_pull(grad_hidden)
    grad_gate_in = grad_gate_raw.astype(narrow)
    grad_up_in = grad_up_raw.astype(narrow)
    grad_mlp_part = rows_dot(grad_gate_in, gate_weight, 1, 0) + rows_dot(
        grad_up_in, up_weight, 1, 0
    )
    (grad_mlp_blocks,) = exchange(
        6,
        "grad_mlp_scatter",
        [
            (
                "scatter",
                ("head",),
                grad_mlp_part.astype(narrow).reshape(head_count, tok_rows, model_width),
            )
        ],
    )
    ff_terms = jnp.concatenate(
        [
            rows_dot(grad_gate_in, mlp_in, 0, 0).reshape(group_count, ff_cols, model_width),
            rows_dot(grad_up_in, mlp_in, 0, 0).reshape(group_count, ff_cols, model_width),
            rows_dot(hidden, grad_down_in, 0, 0).reshape(group_count, ff_cols, model_width),
        ],
        axis=1,
    ).astype(narrow)
    ff_blocks = lax.all_to_all(ff_terms, weight_axes, split_axis=0, concat_axis=0, tiled=True)

    grad_mlp_in = add_up(grad_mlp_blocks)
    grad_mid_part, gain_two = norm_back(middle, inverse_mid, norm_gains[2], grad_mlp_in)
    grad_middle = cot_wide + grad_mid_part
    grad_branch_raw, gain_one = norm_back(branch, inverse_branch, norm_gains[1], grad_middle)
    (grad_branch_blocks,) = exchange(
        7, "grad_branch_gather", [("gather", ("head",), grad_branch_raw.astype(narrow))]
    )
    grad_branch = grad_branch_blocks.reshape(query_rows, model_width)
    head_grad = rows_dot(grad_branch, out_weight, 1, 1).astype(narrow)
    row_delta = jnp.sum(head_grad.astype(jnp.float32) * attn_exact, axis=1, keepdims=True)
    grad_probs = rows_dot(head_grad, all_values, 1, 1)
    grad_scores = (probs_wide * (grad_probs - row_delta)).astype(narrow)
    value_sums = rows_dot(prob_rows, head_grad, 0, 0)
    key_sums = rows_dot(grad_scores, head_query, 0, 0)
    grad_rot_query = rows_dot(grad_scores, all_keys, 1, 0)
    query_back = rotate(grad_rot_query * score_scale, cosine_own, -sine_own)
    grad_query_raw, gain_query = norm_back(query_raw, inverse_query, qk_gains[0], query_back)
    key_back = rotate(key_sums, cosine, -sine_part)
    grad_key_raw, gain_key = norm_back(key_raw, inverse_key, qk_gains[1], key_back)
    grad_query_in = grad_query_raw.astype(narrow)
    grad_key_in = grad_key_raw.astype(narrow)
    grad_value_in = value_sums.astype(narrow)
    grad_attn_part = rows_dot(grad_key_in, key_weight, 1, 0) + rows_dot(
        grad_value_in, value_weight, 1, 0
    )
    own_part = lax.dynamic_slice_in_dim(grad_attn_part, first_query, query_rows) + rows_dot(
        grad_query_in, query_weight, 1, 0
    )
    grad_attn_part = lax.dynamic_update_slice_in_dim(grad_attn_part, own_part, first_query, 0)
    head_terms = jnp.concatenate(
        [
            rows_dot(grad_query_in, attn_in, 0, 0).reshape(group_count, query_cols, model_width),
            rows_dot(attn_out, grad_branch, 0, 0).reshape(group_count, query_cols, model_width),
        ],
        axis=1,
    ).astype(narrow)
    key_value_terms = jnp.concatenate(
        [
            rows_dot(grad_key_in, attn_in_all, 0, 0).reshape(every_count, key_cols, model_width),
            rows_dot(grad_value_in, attn_in_all, 0, 0).reshape(every_count, key_cols, model_width),
        ],
        axis=1,
    ).astype(narrow)
    grad_attn_blocks, head_blocks, key_value_blocks = exchange(
        8,
        "last_scatter",
        [
            (
                "scatter",
                sequence_axes,
                grad_attn_part.astype(narrow).reshape(-1, tok_rows, model_width),
            ),
            ("scatter", weight_axes, head_terms),
            ("scatter", every_axis, key_value_terms),
        ],
        every_axis,
    )
    grad_attn_in = add_up(grad_attn_blocks)
    grad_in_part, gain_zero = norm_back(input_wide, inverse_in, norm_gains[0], grad_attn_in)
    d_block_in = (grad_middle + grad_in_part).astype(narrow)

    pad = ((0, 0), (0, model_width - head_width))
    gain_terms = jnp.concatenate(
        [
            jnp.sum(gain_zero, axis=0, keepdims=True),
            jnp.sum(gain_one, axis=0, keepdims=True),
            jnp.sum(gain_two, axis=0, keepdims=True),
            jnp.sum(gain_three, axis=0, keepdims=True),
            jnp.pad(jnp.sum(gain_query, axis=0, keepdims=True), pad),
            jnp.pad(jnp.sum(gain_key, axis=0, keepdims=True), pad),
            jnp.zeros((2, model_width), jnp.float32),
        ],
        axis=0,
    )
    (gain_blocks,) = exchange(9, "gain_gather", [("gather", every_axis, gain_terms)])
    gains = add_up(gain_blocks)

    head_own = lax.ppermute(add_up(head_blocks).astype(narrow), every_axis, to_owners).astype(
        jnp.float32
    )
    key_value_own = add_up(key_value_blocks)
    ff_own = add_up(ff_blocks)
    return (
        block_out,
        d_block_in,
        gains[:4],
        gains[4:6, :head_width],
        head_own[:query_cols].T,
        key_value_own[:key_cols].T,
        key_value_own[key_cols:].T,
        head_own[query_cols:],
        ff_own[:ff_cols].T,
        ff_own[ff_cols : 2 * ff_cols].T,
        ff_own[2 * ff_cols :],
    )


def solution(mesh):
    in_specs = (
        P(("dp", "ctx", "head"), None),
        P(("dp", "ctx", "head"), None),
        P(("dp", "ctx")),
        P(),
        P(),
        P(None, ("dp", "ctx", "head")),
        P(None, ("dp", "ctx", "head")),
        P(None, ("dp", "ctx", "head")),
        P(("dp", "ctx", "head"), None),
        P(None, ("dp", "ctx", "head")),
        P(None, ("dp", "ctx", "head")),
        P(("dp", "ctx", "head"), None),
    )
    out_specs = (
        P(("dp", "ctx", "head"), None),
        P(("dp", "ctx", "head"), None),
        P(),
        P(),
        P(None, ("dp", "ctx", "head")),
        P(None, ("dp", "ctx", "head")),
        P(None, ("dp", "ctx", "head")),
        P(("dp", "ctx", "head"), None),
        P(None, ("dp", "ctx", "head")),
        P(None, ("dp", "ctx", "head")),
        P(("dp", "ctx", "head"), None),
    )
    return jax.shard_map(local, mesh=mesh, in_specs=in_specs, out_specs=out_specs, check_vma=False)
```

```python
import math

import jax
import jax.numpy as jnp
from jax import lax
from jax.experimental import pallas as pl
from jax.experimental.pallas import tpu as pltpu
from jax.sharding import PartitionSpec as P

epsilon = 1e-06
rope_base = 1000000.0
score_scale = 0.0625
negative_fill = -1e30


def norm_rows(values, gain_vec):
    inverse = lax.rsqrt(jnp.mean(values * values, axis=-1, keepdims=True) + epsilon)
    return (values * inverse * gain_vec, inverse)


def norm_back(values, inverse, gain_vec, upstream):
    scaled = upstream * gain_vec
    inner_mean = jnp.mean(scaled * values, axis=-1, keepdims=True)
    return (
        inverse * scaled - values * (inverse * inverse * inverse) * inner_mean,
        upstream * values * inverse,
    )


def rope_angles(positions, full_width):
    ladder = jnp.arange(full_width // 2, dtype=jnp.float32)
    frequency = jnp.exp(ladder * (-2.0 / full_width) * math.log(rope_base))
    angles = positions.astype(jnp.float32)[:, None] * frequency[None, :]
    return (jnp.cos(angles), jnp.sin(angles))


def rotate(values, cosine, sine_part):
    middle = values.shape[-1] // 2
    first_half = values[..., :middle]
    second = values[..., middle:]
    return jnp.concatenate(
        [first_half * cosine - second * sine_part, second * cosine + first_half * sine_part],
        axis=-1,
    )


def gelu_product(gate_pre, up_pre):
    return jax.nn.gelu(gate_pre, approximate=True) * up_pre


every_axis = ("dp", "ctx", "head")
sequence_axes = ("ctx", "head")
weight_axes = ("dp", "ctx")


def place_in(axes):
    place = 0
    for name in axes:
        place = place * lax.axis_size(name) + lax.axis_index(name)
    return place


def coordinates(axes, place):
    found = {}
    for name in reversed(axes):
        size = lax.axis_size(name)
        found[name] = lax.rem(place, size)
        place = place // size
    return found


def each_peer(count, step):
    if count <= 8:
        for offset in range(1, count):
            step(offset)
    else:

        def looped(offset, carry):
            step(offset)
            return carry

        lax.fori_loop(1, count, looped, 0)


def exchange_kernel(kinds, greet, counts, *refs):
    total = len(kinds)
    sources, targets, sems = refs[:total], refs[total : 2 * total], refs[2 * total :]
    barrier = pltpu.get_barrier_semaphore()
    waits = 0
    for axes, count in greet:
        me = place_in(axes)

        def greet_peer(offset, axes=axes, count=count, me=me):
            pl.semaphore_signal(
                barrier,
                inc=1,
                device_id=coordinates(axes, lax.rem(me + offset, count)),
                device_id_type=pl.DeviceIdType.MESH,
            )

        each_peer(count, greet_peer)
        waits += count - 1
    locals_started = []
    for part, (kind, axes) in enumerate(kinds):
        me = place_in(axes)
        source = sources[part].at[me] if kind == "scatter" else sources[part]
        copy = pltpu.make_async_copy(source, targets[part].at[me], sems[3 * part + 2].at[0])
        copy.start()
        locals_started.append(copy)
    pl.semaphore_wait(barrier, waits)

    def descriptor(part, offset, backward):
        kind, axes = kinds[part]
        count = counts[part]
        me = place_in(axes)
        to = lax.rem(me + offset, count)
        origin = lax.rem(me + count - offset, count) if backward else me
        source = sources[part].at[to] if kind == "scatter" else sources[part]
        return pltpu.make_async_remote_copy(
            src_ref=source,
            dst_ref=targets[part].at[origin],
            send_sem=sems[3 * part].at[offset],
            recv_sem=sems[3 * part + 1].at[origin],
            device_id=coordinates(axes, to),
            device_id_type=pl.DeviceIdType.MESH,
        )

    for part in range(total):
        each_peer(counts[part], lambda offset: descriptor(part, offset, False).start())
    for copy in locals_started:
        copy.wait()
    for part in range(total):
        each_peer(counts[part], lambda offset: descriptor(part, offset, True).wait_recv())
    for part in range(total):
        each_peer(counts[part], lambda offset: descriptor(part, offset, False).wait_send())


def exchange(call_id, name, parts, greet_axes=None):
    kinds = tuple((kind, axes) for kind, axes, _ in parts)
    arrays = [array for _, _, array in parts]
    counts = tuple(lax.axis_size(axes) for _, axes in kinds)
    if greet_axes is None:
        greet_axes = kinds[0][1]
    greet = ((greet_axes, lax.axis_size(greet_axes)),)
    shapes = [
        jax.ShapeDtypeStruct(
            array.shape if kind == "scatter" else (count,) + array.shape, array.dtype
        )
        for (kind, _, array), count in zip(parts, counts)
    ]
    scratch = []
    for count in counts:
        scratch += [
            pltpu.SemaphoreType.DMA((count,)),
            pltpu.SemaphoreType.DMA((count,)),
            pltpu.SemaphoreType.DMA((1,)),
        ]
    in_vmem = pl.BlockSpec(memory_space=pltpu.VMEM)
    return pl.pallas_call(
        lambda *refs: exchange_kernel(kinds, greet, counts, *refs),
        out_shape=shapes,
        in_specs=[in_vmem] * len(arrays),
        out_specs=[in_vmem] * len(arrays),
        scratch_shapes=scratch,
        compiler_params=pltpu.CompilerParams(collective_id=call_id, has_side_effects=True),
        name=name,
    )(*arrays)


def digit_place(digit):
    if digit == "head_slow":
        return lax.axis_index("head") // fast_size()
    if digit == "head_fast":
        return lax.rem(lax.axis_index("head"), fast_size())
    return lax.axis_index(digit)


def fast_size():
    return 2 if lax.axis_size("head") % 2 == 0 else 1


def digit_size(digit):
    if digit == "head_slow":
        return lax.axis_size("head") // fast_size()
    if digit == "head_fast":
        return fast_size()
    return lax.axis_size(digit)


def digit_device(digit, value):
    if digit == "head_slow":
        return {"head": value * fast_size() + digit_place("head_fast")}
    if digit == "head_fast":
        return {"head": digit_place("head_slow") * fast_size() + value}
    return {digit: value}


def staged_kernel(plans, greeted, *refs):
    total = len(plans)
    sources, targets, sems = refs[:total], refs[total : 2 * total], list(refs[2 * total :])
    barrier = pltpu.get_barrier_semaphore()
    waits = 0
    for digit in greeted:
        count, me = digit_size(digit), digit_place(digit)
        for offset in range(1, count):
            pl.semaphore_signal(
                barrier,
                inc=1,
                device_id=digit_device(digit, lax.rem(me + offset, count)),
                device_id_type=pl.DeviceIdType.MESH,
            )
            waits += 1
    local_sems = sems[:total]
    rest = sems[total:]
    pairs = []
    for plan in plans:
        pairs.append([(rest.pop(0), rest.pop(0)) for _ in plan])
    own = []
    for part, plan in enumerate(plans):
        here = tuple(digit_place(digit) for digit in reversed(plan))
        copy = pltpu.make_async_copy(sources[part], targets[part].at[here], local_sems[part].at[0])
        copy.start()
        own.append(copy)
    pl.semaphore_wait(barrier, waits)

    def descriptors(part, turn, backward):
        plan = plans[part]
        digit = plan[turn]
        count, me = digit_size(digit), digit_place(digit)
        outer = tuple(digit_place(name) for name in reversed(plan[turn + 1 :]))
        found = []
        for offset in range(1, count):
            to = lax.rem(me + offset, count)
            origin = lax.rem(me + count - offset, count) if backward else me
            source = sources[part] if turn == 0 else targets[part].at[outer + (me,)]
            found.append(
                pltpu.make_async_remote_copy(
                    src_ref=source,
                    dst_ref=targets[part].at[outer + (origin,)],
                    send_sem=pairs[part][turn][0].at[offset],
                    recv_sem=pairs[part][turn][1].at[origin],
                    device_id=digit_device(digit, to),
                    device_id_type=pl.DeviceIdType.MESH,
                )
            )
        return found

    most = max(len(plan) for plan in plans)
    for turn in range(most + 1):
        for part, plan in enumerate(plans):
            if 0 < turn <= len(plan):
                for copy in descriptors(part, turn - 1, True):
                    copy.wait_recv()
            if turn == 1:
                own[part].wait()
            if turn < len(plan):
                for copy in descriptors(part, turn, False):
                    copy.start()
    for part, plan in enumerate(plans):
        for turn in range(len(plan)):
            for copy in descriptors(part, turn, False):
                copy.wait_send()


def staged_gather(call_id, name, parts):
    plans = [plan for plan, _ in parts]
    arrays = [array for _, array in parts]
    greeted = []
    for plan in plans:
        greeted += [digit for digit in plan if digit not in greeted]
    shapes = [
        jax.ShapeDtypeStruct(
            tuple(digit_size(digit) for digit in reversed(plan)) + array.shape, array.dtype
        )
        for plan, array in parts
    ]
    scratch = [pltpu.SemaphoreType.DMA((1,)) for _ in parts]
    for plan in plans:
        for digit in plan:
            scratch += [pltpu.SemaphoreType.DMA((digit_size(digit),))] * 2
    in_vmem = pl.BlockSpec(memory_space=pltpu.VMEM)
    return pl.pallas_call(
        lambda *refs: staged_kernel(plans, greeted, *refs),
        out_shape=shapes,
        in_specs=[in_vmem] * len(arrays),
        out_specs=[in_vmem] * len(arrays),
        scratch_shapes=scratch,
        compiler_params=pltpu.CompilerParams(collective_id=call_id, has_side_effects=True),
        name=name,
    )(*arrays)


def gather_rows(call_id, name, rows):
    (blocks,) = staged_gather(call_id, name, [(("head_slow", "head_fast"), rows)])
    return jnp.swapaxes(blocks, 0, 1).reshape(-1, rows.shape[1])


def shifted(array, axis, offset):
    count = lax.axis_size(axis)
    return lax.ppermute(array, axis, [(here, (here + offset) % count) for here in range(count)])


def gelu_parts(value):
    root = math.sqrt(2.0 / math.pi)
    square = value * value
    tanh_part = jnp.tanh(root * (value + 0.044715 * value * square))
    gelu = 0.5 * value * (1.0 + tanh_part)
    slope = 0.5 * (1.0 + tanh_part) + 0.5 * value * (1.0 - tanh_part * tanh_part) * root * (
        1.0 + 3.0 * 0.044715 * square
    )
    return gelu, slope


def mlp_forward_kernel(rows_ref, gate_ref, up_ref, down_ref, gate_pre_ref, up_pre_ref, hidden_ref, part_ref):
    rows = rows_ref[...]
    gate_pre = rows_dot(rows, gate_ref[...], 1, 1)
    up_pre = rows_dot(rows, up_ref[...], 1, 1)
    gate_pre_ref[...] = gate_pre
    up_pre_ref[...] = up_pre
    hidden = (gelu_parts(gate_pre)[0] * up_pre).astype(jnp.bfloat16)
    hidden_ref[...] = hidden
    part_ref[...] = rows_dot(hidden, down_ref[...], 1, 0).astype(jnp.bfloat16)


def mlp_backward_kernel(
    rows_ref, gate_ref, up_ref, down_ref, gate_pre_ref, up_pre_ref, grad_gate_ref, grad_up_ref, part_ref
):
    grad_hidden = rows_dot(rows_ref[...], down_ref[...], 1, 1)
    gelu, slope = gelu_parts(gate_pre_ref[...])
    grad_gate = (grad_hidden * up_pre_ref[...] * slope).astype(jnp.bfloat16)
    grad_up = (grad_hidden * gelu).astype(jnp.bfloat16)
    grad_gate_ref[...] = grad_gate
    grad_up_ref[...] = grad_up
    part_ref[...] = (
        rows_dot(grad_gate, gate_ref[...], 1, 0) + rows_dot(grad_up, up_ref[...], 1, 0)
    ).astype(jnp.bfloat16)


def rows_dot(left, right, left_dim, right_dim):
    return lax.dot_general(
        left, right, (((left_dim,), (right_dim,)), ((), ())), preferred_element_type=jnp.float32
    )


def add_up(blocks):
    return jnp.sum(blocks.astype(jnp.float32), axis=0)


def local(
    block_in,
    cotangent,
    positions,
    norm_gains,
    qk_gains,
    w_query,
    w_key,
    w_value,
    w_out,
    w_gate,
    w_up,
    w_down,
):
    tok_rows, model_width = block_in.shape
    head_count = lax.axis_size("head")
    head_width = qk_gains.shape[1]
    ctx_slot = lax.axis_index("ctx")
    query_rows = head_count * tok_rows
    group_count = lax.axis_size(weight_axes)
    every_count = lax.axis_size(every_axis)
    length_all = lax.axis_size(sequence_axes) * tok_rows
    query_cols = w_query.shape[1]
    key_cols = w_key.shape[1]
    ff_cols = w_gate.shape[1]
    narrow = jnp.bfloat16

    ff_rows = jnp.concatenate([w_gate.T, w_up.T, w_down], axis=0)
    dp_count, ctx_count = lax.axis_size("dp"), lax.axis_size("ctx")
    near_blocks = [ff_rows] + [shifted(ff_rows, "dp", offset) for offset in range(1, dp_count)]
    ff_slots = list(near_blocks)
    for offset in range(1, ctx_count):
        ff_slots += [shifted(block, "ctx", offset) for block in near_blocks]

    to_heads = [
        (head * group_count + index, index * head_count + head)
        for head in range(head_count)
        for index in range(group_count)
    ]
    to_owners = [(there, here) for here, there in to_heads]
    head_rows = lax.ppermute(
        jnp.concatenate([w_query.T, w_out], axis=0), every_axis, to_heads
    )
    key_value_rows = jnp.concatenate([w_key.T, w_value.T], axis=0)
    block_all, key_value_all, head_all, position_all = staged_gather(
        1,
        "first_gather",
        [
            (("ctx", "head_slow", "head_fast"), block_in),
            (("dp", "ctx", "head_slow", "head_fast"), key_value_rows),
            (("dp", "ctx"), head_rows),
            (("ctx",), positions.reshape(-1, 128)),
        ],
    )
    block_all = block_all.transpose(2, 1, 0, 3, 4)
    key_value_all = key_value_all.transpose(3, 2, 1, 0, 4, 5).reshape(
        every_count, 2 * key_cols, model_width
    )
    head_all = head_all.transpose(1, 0, 2, 3).reshape(group_count, 2 * query_cols, model_width)
    query_weight = head_all[:, :query_cols].reshape(head_width, model_width)
    out_weight = head_all[:, query_cols:].reshape(head_width, model_width)
    key_weight = key_value_all[:, :key_cols].reshape(head_width, model_width)
    value_weight = key_value_all[:, key_cols:].reshape(head_width, model_width)

    input_all = block_all.reshape(length_all, model_width).astype(jnp.float32)
    attn_in_all = norm_rows(input_all, norm_gains[0])[0].astype(narrow)
    first_query = ctx_slot * query_rows
    attn_in = lax.dynamic_slice_in_dim(attn_in_all, first_query, query_rows)
    query_raw = rows_dot(attn_in, query_weight, 1, 1)
    key_raw = rows_dot(attn_in_all, key_weight, 1, 1)
    all_values = rows_dot(attn_in_all, value_weight, 1, 1).astype(narrow)
    query_normed, inverse_query = norm_rows(query_raw, qk_gains[0])
    key_normed, inverse_key = norm_rows(key_raw, qk_gains[1])
    cosine, sine_part = rope_angles(position_all.reshape(length_all), head_width)
    cosine_own = lax.dynamic_slice_in_dim(cosine, first_query, query_rows)
    sine_own = lax.dynamic_slice_in_dim(sine_part, first_query, query_rows)
    head_query = (rotate(query_normed, cosine_own, sine_own) * score_scale).astype(narrow)
    all_keys = rotate(key_normed, cosine, sine_part).astype(narrow)

    query_index = first_query + jnp.arange(query_rows, dtype=jnp.int32)
    lowest_key = query_index - positions
    key_index = jnp.arange(length_all, dtype=jnp.int32)
    visible = (key_index[None, :] <= query_index[:, None]) & (
        key_index[None, :] >= lowest_key[:, None]
    )
    scores = jnp.where(visible, rows_dot(head_query, all_keys, 1, 1), negative_fill)
    top = jnp.max(scores, axis=1, keepdims=True)
    log_total = top + jnp.log(jnp.sum(jnp.exp(scores - top), axis=1, keepdims=True))
    probs_wide = jnp.exp(scores - log_total)
    prob_rows = probs_wide.astype(narrow)
    attn_exact = rows_dot(prob_rows, all_values, 1, 0)
    attn_out = attn_exact.astype(narrow)
    branch_part = rows_dot(attn_out, out_weight, 1, 0).astype(narrow)
    (branch_blocks,) = exchange(
        2,
        "branch_scatter",
        [("scatter", ("head",), branch_part.reshape(head_count, tok_rows, model_width))],
    )
    branch = add_up(branch_blocks)
    input_wide = block_in.astype(jnp.float32)
    inverse_in = norm_rows(input_wide, norm_gains[0])[1]
    branch_normed, inverse_branch = norm_rows(branch, norm_gains[1])
    middle = input_wide + branch_normed
    mlp_norm, inverse_mid = norm_rows(middle, norm_gains[2])
    mlp_in = gather_rows(3, "mlp_gather", mlp_norm.astype(narrow))

    ff_width = group_count * ff_cols
    gate_weight = jnp.concatenate([block[:ff_cols] for block in ff_slots], axis=0)
    up_weight = jnp.concatenate([block[ff_cols : 2 * ff_cols] for block in ff_slots], axis=0)
    down_weight = jnp.concatenate([block[2 * ff_cols :] for block in ff_slots], axis=0)
    wide_ff = jax.ShapeDtypeStruct((query_rows, ff_width), jnp.float32)
    narrow_ff = jax.ShapeDtypeStruct((query_rows, ff_width), narrow)
    narrow_rows = jax.ShapeDtypeStruct((query_rows, model_width), narrow)
    gate_pre, up_pre, hidden, down_part = pl.pallas_call(
        mlp_forward_kernel,
        out_shape=[wide_ff, wide_ff, narrow_ff, narrow_rows],
        name="mlp_forward",
    )(mlp_in, gate_weight, up_weight, down_weight)
    (down_blocks,) = exchange(
        4,
        "down_scatter",
        [("scatter", ("head",), down_part.reshape(head_count, tok_rows, model_width))],
    )
    down_raw = add_up(down_blocks)
    down_normed, inverse_down = norm_rows(down_raw, norm_gains[3])
    block_out = (middle + down_normed).astype(narrow)
    cot_wide = cotangent.astype(jnp.float32)
    grad_down_raw, gain_three = norm_back(down_raw, inverse_down, norm_gains[3], cot_wide)
    grad_down_in = gather_rows(5, "grad_down_gather", grad_down_raw.astype(narrow))
    grad_gate_in, grad_up_in, grad_mlp_part = pl.pallas_call(
        mlp_backward_kernel,
        out_shape=[narrow_ff, narrow_ff, narrow_rows],
        name="mlp_backward",
    )(grad_down_in, gate_weight, up_weight, down_weight, gate_pre, up_pre)
    (grad_mlp_blocks,) = exchange(
        6,
        "grad_mlp_scatter",
        [
            (
                "scatter",
                ("head",),
                grad_mlp_part.reshape(head_count, tok_rows, model_width),
            )
        ],
    )
    slots = (ctx_count, dp_count, ff_cols, model_width)
    ff_terms = jnp.concatenate(
        [
            rows_dot(grad_gate_in, mlp_in, 0, 0).astype(narrow).reshape(slots),
            rows_dot(grad_up_in, mlp_in, 0, 0).astype(narrow).reshape(slots),
            rows_dot(hidden, grad_down_in, 0, 0).astype(narrow).reshape(slots),
        ],
        axis=2,
    )
    ff_sums = ff_terms[0].astype(jnp.float32)
    for offset in range(1, ctx_count):
        ff_sums = ff_sums + shifted(ff_terms[offset], "ctx", -offset).astype(jnp.float32)
    ff_own = ff_sums[0]
    for offset in range(1, dp_count):
        ff_own = ff_own + shifted(ff_sums[offset].astype(narrow), "dp", -offset).astype(
            jnp.float32
        )

    grad_mlp_in = add_up(grad_mlp_blocks)
    grad_mid_part, gain_two = norm_back(middle, inverse_mid, norm_gains[2], grad_mlp_in)
    grad_middle = cot_wide + grad_mid_part
    grad_branch_raw, gain_one = norm_back(branch, inverse_branch, norm_gains[1], grad_middle)
    grad_branch = gather_rows(7, "grad_branch_gather", grad_branch_raw.astype(narrow))
    head_grad = rows_dot(grad_branch, out_weight, 1, 1).astype(narrow)
    row_delta = jnp.sum(head_grad.astype(jnp.float32) * attn_exact, axis=1, keepdims=True)
    grad_probs = rows_dot(head_grad, all_values, 1, 1)
    grad_scores = (probs_wide * (grad_probs - row_delta)).astype(narrow)
    value_sums = rows_dot(prob_rows, head_grad, 0, 0)
    key_sums = rows_dot(grad_scores, head_query, 0, 0)
    grad_rot_query = rows_dot(grad_scores, all_keys, 1, 0)
    query_back = rotate(grad_rot_query * score_scale, cosine_own, -sine_own)
    grad_query_raw, gain_query = norm_back(query_raw, inverse_query, qk_gains[0], query_back)
    key_back = rotate(key_sums, cosine, -sine_part)
    grad_key_raw, gain_key = norm_back(key_raw, inverse_key, qk_gains[1], key_back)
    grad_query_in = grad_query_raw.astype(narrow)
    grad_key_in = grad_key_raw.astype(narrow)
    grad_value_in = value_sums.astype(narrow)
    grad_attn_part = rows_dot(grad_key_in, key_weight, 1, 0) + rows_dot(
        grad_value_in, value_weight, 1, 0
    )
    own_part = lax.dynamic_slice_in_dim(grad_attn_part, first_query, query_rows) + rows_dot(
        grad_query_in, query_weight, 1, 0
    )
    grad_attn_part = lax.dynamic_update_slice_in_dim(grad_attn_part, own_part, first_query, 0)
    head_terms = jnp.concatenate(
        [
            rows_dot(grad_query_in, attn_in, 0, 0).reshape(group_count, query_cols, model_width),
            rows_dot(attn_out, grad_branch, 0, 0).reshape(group_count, query_cols, model_width),
        ],
        axis=1,
    ).astype(narrow)
    planes = (dp_count, every_count // dp_count, key_cols, model_width)
    key_value_terms = jnp.concatenate(
        [
            rows_dot(grad_key_in, attn_in_all, 0, 0).reshape(planes),
            rows_dot(grad_value_in, attn_in_all, 0, 0).reshape(planes),
        ],
        axis=2,
    ).astype(narrow).transpose(1, 0, 2, 3)
    head_terms = head_terms.reshape(dp_count, ctx_count, 2 * query_cols, model_width)
    grad_attn_blocks, head_blocks, key_value_blocks = exchange(
        8,
        "last_scatter",
        [
            (
                "scatter",
                sequence_axes,
                grad_attn_part.astype(narrow).reshape(-1, tok_rows, model_width),
            ),
            ("scatter", ("ctx",), head_terms.transpose(1, 0, 2, 3)),
            ("scatter", sequence_axes, key_value_terms),
        ],
        sequence_axes,
    )
    grad_attn_in = add_up(grad_attn_blocks)
    grad_in_part, gain_zero = norm_back(input_wide, inverse_in, norm_gains[0], grad_attn_in)
    d_block_in = (grad_middle + grad_in_part).astype(narrow)

    pad = ((0, 0), (0, model_width - head_width))
    gain_terms = jnp.concatenate(
        [
            jnp.sum(gain_zero, axis=0, keepdims=True),
            jnp.sum(gain_one, axis=0, keepdims=True),
            jnp.sum(gain_two, axis=0, keepdims=True),
            jnp.sum(gain_three, axis=0, keepdims=True),
            jnp.pad(jnp.sum(gain_query, axis=0, keepdims=True), pad),
            jnp.pad(jnp.sum(gain_key, axis=0, keepdims=True), pad),
            jnp.zeros((2, model_width), jnp.float32),
        ],
        axis=0,
    )
    gain_blocks, head_blocks, key_value_blocks = exchange(
        9,
        "depth_exchange",
        [
            ("gather", ("dp",), gain_terms),
            ("scatter", ("dp",), add_up(head_blocks).astype(narrow)),
            ("scatter", ("dp",), add_up(key_value_blocks).astype(narrow)),
        ],
    )
    head_own = lax.ppermute(add_up(head_blocks).astype(narrow), every_axis, to_owners).astype(
        jnp.float32
    )
    (gain_blocks,) = exchange(10, "gain_gather", [("gather", sequence_axes, add_up(gain_blocks))])
    gains = add_up(gain_blocks)
    key_value_own = add_up(key_value_blocks)
    return (
        block_out,
        d_block_in,
        gains[:4],
        gains[4:6, :head_width],
        head_own[:query_cols].T,
        key_value_own[:key_cols].T,
        key_value_own[key_cols:].T,
        head_own[query_cols:],
        ff_own[:ff_cols].T,
        ff_own[ff_cols : 2 * ff_cols].T,
        ff_own[2 * ff_cols :],
    )


def solution(mesh):
    in_specs = (
        P(("dp", "ctx", "head"), None),
        P(("dp", "ctx", "head"), None),
        P(("dp", "ctx")),
        P(),
        P(),
        P(None, ("dp", "ctx", "head")),
        P(None, ("dp", "ctx", "head")),
        P(None, ("dp", "ctx", "head")),
        P(("dp", "ctx", "head"), None),
        P(None, ("dp", "ctx", "head")),
        P(None, ("dp", "ctx", "head")),
        P(("dp", "ctx", "head"), None),
    )
    out_specs = (
        P(("dp", "ctx", "head"), None),
        P(("dp", "ctx", "head"), None),
        P(),
        P(),
        P(None, ("dp", "ctx", "head")),
        P(None, ("dp", "ctx", "head")),
        P(None, ("dp", "ctx", "head")),
        P(("dp", "ctx", "head"), None),
        P(None, ("dp", "ctx", "head")),
        P(None, ("dp", "ctx", "head")),
        P(("dp", "ctx", "head"), None),
    )
    return jax.shard_map(local, mesh=mesh, in_specs=in_specs, out_specs=out_specs, check_vma=False)
```

```python
import math

import jax
import jax.numpy as jnp
from jax import lax
from jax.experimental import pallas as pl
from jax.experimental.pallas import tpu as pltpu
from jax.sharding import PartitionSpec as P

epsilon = 1e-06
rope_base = 1000000.0
score_scale = 0.0625
negative_fill = -1e30


def norm_rows(values, gain_vec):
    inverse = lax.rsqrt(jnp.mean(values * values, axis=-1, keepdims=True) + epsilon)
    return (values * inverse * gain_vec, inverse)


def norm_back(values, inverse, gain_vec, upstream):
    scaled = upstream * gain_vec
    inner_mean = jnp.mean(scaled * values, axis=-1, keepdims=True)
    return (
        inverse * scaled - values * (inverse * inverse * inverse) * inner_mean,
        upstream * values * inverse,
    )


def rope_angles(positions, full_width):
    ladder = jnp.arange(full_width // 2, dtype=jnp.float32)
    frequency = jnp.exp(ladder * (-2.0 / full_width) * math.log(rope_base))
    angles = positions.astype(jnp.float32)[:, None] * frequency[None, :]
    return (jnp.cos(angles), jnp.sin(angles))


def rotate(values, cosine, sine_part):
    middle = values.shape[-1] // 2
    first_half = values[..., :middle]
    second = values[..., middle:]
    return jnp.concatenate(
        [first_half * cosine - second * sine_part, second * cosine + first_half * sine_part],
        axis=-1,
    )


def gelu_product(gate_pre, up_pre):
    return jax.nn.gelu(gate_pre, approximate=True) * up_pre


every_axis = ("dp", "ctx", "head")
sequence_axes = ("ctx", "head")
weight_axes = ("dp", "ctx")


def place_in(axes):
    place = 0
    for name in axes:
        place = place * lax.axis_size(name) + lax.axis_index(name)
    return place


def coordinates(axes, place):
    found = {}
    for name in reversed(axes):
        size = lax.axis_size(name)
        found[name] = lax.rem(place, size)
        place = place // size
    return found


def each_peer(count, step):
    if count <= 8:
        for offset in range(1, count):
            step(offset)
    else:

        def looped(offset, carry):
            step(offset)
            return carry

        lax.fori_loop(1, count, looped, 0)


def exchange_kernel(kinds, greet, counts, *refs):
    total = len(kinds)
    sources, targets, sems = refs[:total], refs[total : 2 * total], refs[2 * total :]
    barrier = pltpu.get_barrier_semaphore()
    waits = 0
    for axes, count in greet:
        me = place_in(axes)

        def greet_peer(offset, axes=axes, count=count, me=me):
            pl.semaphore_signal(
                barrier,
                inc=1,
                device_id=coordinates(axes, lax.rem(me + offset, count)),
                device_id_type=pl.DeviceIdType.MESH,
            )

        each_peer(count, greet_peer)
        waits += count - 1
    locals_started = []
    for part, (kind, axes) in enumerate(kinds):
        me = place_in(axes)
        source = {"scatter": me, "relative": 0}.get(kind)
        source = sources[part] if source is None else sources[part].at[source]
        copy = pltpu.make_async_copy(source, targets[part].at[me], sems[3 * part + 2].at[0])
        copy.start()
        locals_started.append(copy)
    pl.semaphore_wait(barrier, waits)

    def descriptor(part, offset, backward):
        kind, axes = kinds[part]
        count = counts[part]
        me = place_in(axes)
        to = lax.rem(me + offset, count)
        origin = lax.rem(me + count - offset, count) if backward else me
        source = {"scatter": to, "relative": lax.rem(count - offset, count)}.get(kind)
        source = sources[part] if source is None else sources[part].at[source]
        return pltpu.make_async_remote_copy(
            src_ref=source,
            dst_ref=targets[part].at[origin],
            send_sem=sems[3 * part].at[offset],
            recv_sem=sems[3 * part + 1].at[origin],
            device_id=coordinates(axes, to),
            device_id_type=pl.DeviceIdType.MESH,
        )

    for part in range(total):
        each_peer(counts[part], lambda offset: descriptor(part, offset, False).start())
    for copy in locals_started:
        copy.wait()
    for part in range(total):
        each_peer(counts[part], lambda offset: descriptor(part, offset, True).wait_recv())
    for part in range(total):
        each_peer(counts[part], lambda offset: descriptor(part, offset, False).wait_send())


def exchange(call_id, name, parts, greet_axes=None):
    kinds = tuple((kind, axes) for kind, axes, _ in parts)
    arrays = [array for _, _, array in parts]
    counts = tuple(lax.axis_size(axes) for _, axes in kinds)
    if greet_axes is None:
        greet_axes = (kinds[0][1],)
    greet = tuple((axes, lax.axis_size(axes)) for axes in greet_axes)
    shapes = [
        jax.ShapeDtypeStruct(
            (count,) + array.shape if kind == "gather" else array.shape, array.dtype
        )
        for (kind, _, array), count in zip(parts, counts)
    ]
    scratch = []
    for count in counts:
        scratch += [
            pltpu.SemaphoreType.DMA((count,)),
            pltpu.SemaphoreType.DMA((count,)),
            pltpu.SemaphoreType.DMA((1,)),
        ]
    in_vmem = pl.BlockSpec(memory_space=pltpu.VMEM)
    return pl.pallas_call(
        lambda *refs: exchange_kernel(kinds, greet, counts, *refs),
        out_shape=shapes,
        in_specs=[in_vmem] * len(arrays),
        out_specs=[in_vmem] * len(arrays),
        scratch_shapes=scratch,
        compiler_params=pltpu.CompilerParams(collective_id=call_id, has_side_effects=True),
        name=name,
    )(*arrays)


def digit_place(digit):
    if digit == "head_slow":
        return lax.axis_index("head") // fast_size()
    if digit == "head_fast":
        return lax.rem(lax.axis_index("head"), fast_size())
    return lax.axis_index(digit)


def fast_size():
    return 2 if lax.axis_size("head") % 2 == 0 else 1


def digit_size(digit):
    if digit == "head_slow":
        return lax.axis_size("head") // fast_size()
    if digit == "head_fast":
        return fast_size()
    return lax.axis_size(digit)


def digit_device(digit, value):
    if digit == "head_slow":
        return {"head": value * fast_size() + digit_place("head_fast")}
    if digit == "head_fast":
        return {"head": digit_place("head_slow") * fast_size() + value}
    return {digit: value}


def staged_kernel(plans, greeted, *refs):
    total = len(plans)
    sources, targets, sems = refs[:total], refs[total : 2 * total], list(refs[2 * total :])
    barrier = pltpu.get_barrier_semaphore()
    waits = 0
    for digit in greeted:
        count, me = digit_size(digit), digit_place(digit)
        for offset in range(1, count):
            pl.semaphore_signal(
                barrier,
                inc=1,
                device_id=digit_device(digit, lax.rem(me + offset, count)),
                device_id_type=pl.DeviceIdType.MESH,
            )
            waits += 1
    local_sems = sems[:total]
    rest = sems[total:]
    pairs = []
    for plan in plans:
        pairs.append([(rest.pop(0), rest.pop(0)) for _ in plan])
    own = []
    for part, plan in enumerate(plans):
        here = tuple(digit_place(digit) for digit in reversed(plan))
        copy = pltpu.make_async_copy(sources[part], targets[part].at[here], local_sems[part].at[0])
        copy.start()
        own.append(copy)
    pl.semaphore_wait(barrier, waits)

    def descriptors(part, turn, backward):
        plan = plans[part]
        digit = plan[turn]
        count, me = digit_size(digit), digit_place(digit)
        outer = tuple(digit_place(name) for name in reversed(plan[turn + 1 :]))
        found = []
        for offset in range(1, count):
            to = lax.rem(me + offset, count)
            origin = lax.rem(me + count - offset, count) if backward else me
            source = sources[part] if turn == 0 else targets[part].at[outer + (me,)]
            found.append(
                pltpu.make_async_remote_copy(
                    src_ref=source,
                    dst_ref=targets[part].at[outer + (origin,)],
                    send_sem=pairs[part][turn][0].at[offset],
                    recv_sem=pairs[part][turn][1].at[origin],
                    device_id=digit_device(digit, to),
                    device_id_type=pl.DeviceIdType.MESH,
                )
            )
        return found

    most = max(len(plan) for plan in plans)
    for turn in range(most + 1):
        for part, plan in enumerate(plans):
            if 0 < turn <= len(plan):
                for copy in descriptors(part, turn - 1, True):
                    copy.wait_recv()
            if turn == 1:
                own[part].wait()
            if turn < len(plan):
                for copy in descriptors(part, turn, False):
                    copy.start()
    for part, plan in enumerate(plans):
        for turn in range(len(plan)):
            for copy in descriptors(part, turn, False):
                copy.wait_send()


def staged_gather(call_id, name, parts):
    plans = [plan for plan, _ in parts]
    arrays = [array for _, array in parts]
    greeted = []
    for plan in plans:
        greeted += [digit for digit in plan if digit not in greeted]
    shapes = [
        jax.ShapeDtypeStruct(
            tuple(digit_size(digit) for digit in reversed(plan)) + array.shape, array.dtype
        )
        for plan, array in parts
    ]
    scratch = [pltpu.SemaphoreType.DMA((1,)) for _ in parts]
    for plan in plans:
        for digit in plan:
            scratch += [pltpu.SemaphoreType.DMA((digit_size(digit),))] * 2
    in_vmem = pl.BlockSpec(memory_space=pltpu.VMEM)
    return pl.pallas_call(
        lambda *refs: staged_kernel(plans, greeted, *refs),
        out_shape=shapes,
        in_specs=[in_vmem] * len(arrays),
        out_specs=[in_vmem] * len(arrays),
        scratch_shapes=scratch,
        compiler_params=pltpu.CompilerParams(collective_id=call_id, has_side_effects=True),
        name=name,
    )(*arrays)


def gather_rows(call_id, name, rows):
    (blocks,) = exchange(call_id, name, [("gather", ("head",), rows)])
    return blocks.reshape(-1, rows.shape[1])


def shifted(array, axis, offset):
    count = lax.axis_size(axis)
    return lax.ppermute(array, axis, [(here, (here + offset) % count) for here in range(count)])


def gelu_parts(value):
    root = math.sqrt(2.0 / math.pi)
    square = value * value
    tanh_part = jnp.tanh(root * (value + 0.044715 * value * square))
    gelu = 0.5 * value * (1.0 + tanh_part)
    slope = 0.5 * (1.0 + tanh_part) + 0.5 * value * (1.0 - tanh_part * tanh_part) * root * (
        1.0 + 3.0 * 0.044715 * square
    )
    return gelu, slope


def mlp_forward_kernel(rows_ref, gate_ref, up_ref, down_ref, gate_pre_ref, up_pre_ref, hidden_ref, part_ref):
    rows = rows_ref[...]
    gate_pre = rows_dot(rows, gate_ref[...], 1, 1)
    up_pre = rows_dot(rows, up_ref[...], 1, 1)
    gate_pre_ref[...] = gate_pre
    up_pre_ref[...] = up_pre
    hidden = (gelu_parts(gate_pre)[0] * up_pre).astype(jnp.bfloat16)
    hidden_ref[...] = hidden
    part_ref[...] = rows_dot(hidden, down_ref[...], 1, 0).astype(jnp.bfloat16)


def mlp_backward_kernel(
    rows_ref, gate_ref, up_ref, down_ref, gate_pre_ref, up_pre_ref, grad_gate_ref, grad_up_ref, part_ref
):
    grad_hidden = rows_dot(rows_ref[...], down_ref[...], 1, 1)
    gelu, slope = gelu_parts(gate_pre_ref[...])
    grad_gate = (grad_hidden * up_pre_ref[...] * slope).astype(jnp.bfloat16)
    grad_up = (grad_hidden * gelu).astype(jnp.bfloat16)
    grad_gate_ref[...] = grad_gate
    grad_up_ref[...] = grad_up
    part_ref[...] = (
        rows_dot(grad_gate, gate_ref[...], 1, 0) + rows_dot(grad_up, up_ref[...], 1, 0)
    ).astype(jnp.bfloat16)


def rows_dot(left, right, left_dim, right_dim):
    return lax.dot_general(
        left, right, (((left_dim,), (right_dim,)), ((), ())), preferred_element_type=jnp.float32
    )


def add_up(blocks):
    return jnp.sum(blocks.astype(jnp.float32), axis=0)


def local(
    block_in,
    cotangent,
    positions,
    norm_gains,
    qk_gains,
    w_query,
    w_key,
    w_value,
    w_out,
    w_gate,
    w_up,
    w_down,
):
    tok_rows, model_width = block_in.shape
    head_count = lax.axis_size("head")
    head_width = qk_gains.shape[1]
    ctx_slot = lax.axis_index("ctx")
    query_rows = head_count * tok_rows
    group_count = lax.axis_size(weight_axes)
    every_count = lax.axis_size(every_axis)
    length_all = lax.axis_size(sequence_axes) * tok_rows
    query_cols = w_query.shape[1]
    key_cols = w_key.shape[1]
    ff_cols = w_gate.shape[1]
    narrow = jnp.bfloat16

    ff_rows = jnp.concatenate([w_gate.T, w_up.T, w_down], axis=0)
    dp_count, ctx_count = lax.axis_size("dp"), lax.axis_size("ctx")

    to_heads = [
        (head * group_count + index, index * head_count + head)
        for head in range(head_count)
        for index in range(group_count)
    ]
    to_owners = [(there, here) for here, there in to_heads]
    head_rows = lax.ppermute(
        jnp.concatenate([w_query.T, w_out], axis=0), every_axis, to_heads
    )
    key_value_rows = jnp.concatenate([w_key.T, w_value.T], axis=0)
    block_all, key_value_all, head_all, position_all = staged_gather(
        1,
        "first_gather",
        [
            (("ctx", "head_slow", "head_fast"), block_in),
            (("dp", "ctx", "head_slow", "head_fast"), key_value_rows),
            (("dp", "ctx"), head_rows),
            (("ctx",), positions.reshape(-1, 128)),
        ],
    )
    block_all, ff_rows = lax.optimization_barrier((block_all, ff_rows))
    near_blocks = [ff_rows] + [shifted(ff_rows, "dp", offset) for offset in range(1, dp_count)]
    ff_across = [shifted(ff_rows, "ctx", offset) for offset in range(1, ctx_count)]
    block_all = block_all.transpose(2, 1, 0, 3, 4)
    key_value_all = key_value_all.transpose(3, 2, 1, 0, 4, 5).reshape(
        every_count, 2 * key_cols, model_width
    )
    head_all = head_all.transpose(1, 0, 2, 3).reshape(group_count, 2 * query_cols, model_width)
    query_weight = head_all[:, :query_cols].reshape(head_width, model_width)
    out_weight = head_all[:, query_cols:].reshape(head_width, model_width)
    key_weight = key_value_all[:, :key_cols].reshape(head_width, model_width)
    value_weight = key_value_all[:, key_cols:].reshape(head_width, model_width)

    input_all = block_all.reshape(length_all, model_width).astype(jnp.float32)
    attn_in_all = norm_rows(input_all, norm_gains[0])[0].astype(narrow)
    first_query = ctx_slot * query_rows
    attn_in = lax.dynamic_slice_in_dim(attn_in_all, first_query, query_rows)
    query_raw = rows_dot(attn_in, query_weight, 1, 1)
    key_raw = rows_dot(attn_in_all, key_weight, 1, 1)
    all_values = rows_dot(attn_in_all, value_weight, 1, 1).astype(narrow)
    query_normed, inverse_query = norm_rows(query_raw, qk_gains[0])
    key_normed, inverse_key = norm_rows(key_raw, qk_gains[1])
    cosine, sine_part = rope_angles(position_all.reshape(length_all), head_width)
    cosine_own = lax.dynamic_slice_in_dim(cosine, first_query, query_rows)
    sine_own = lax.dynamic_slice_in_dim(sine_part, first_query, query_rows)
    head_query = (rotate(query_normed, cosine_own, sine_own) * score_scale).astype(narrow)
    all_keys = rotate(key_normed, cosine, sine_part).astype(narrow)

    query_index = first_query + jnp.arange(query_rows, dtype=jnp.int32)
    lowest_key = query_index - positions
    key_index = jnp.arange(length_all, dtype=jnp.int32)
    visible = (key_index[None, :] <= query_index[:, None]) & (
        key_index[None, :] >= lowest_key[:, None]
    )
    scores = jnp.where(visible, rows_dot(head_query, all_keys, 1, 1), negative_fill)
    top = jnp.max(scores, axis=1, keepdims=True)
    log_total = top + jnp.log(jnp.sum(jnp.exp(scores - top), axis=1, keepdims=True))
    probs_wide = jnp.exp(scores - log_total)
    prob_rows = probs_wide.astype(narrow)
    attn_exact = rows_dot(prob_rows, all_values, 1, 0)
    attn_out = attn_exact.astype(narrow)
    branch_part = rows_dot(attn_out, out_weight, 1, 0).astype(narrow)
    (branch_blocks,) = exchange(
        2,
        "branch_scatter",
        [("scatter", ("head",), branch_part.reshape(head_count, tok_rows, model_width))],
    )
    branch = add_up(branch_blocks)
    input_wide = block_in.astype(jnp.float32)
    inverse_in = norm_rows(input_wide, norm_gains[0])[1]
    branch_normed, inverse_branch = norm_rows(branch, norm_gains[1])
    middle = input_wide + branch_normed
    mlp_norm, inverse_mid = norm_rows(middle, norm_gains[2])
    mlp_norm, near_blocks, ff_across = lax.optimization_barrier((mlp_norm, near_blocks, ff_across))
    ff_slots = list(near_blocks)
    for offset in range(1, ctx_count):
        ff_slots += [ff_across[offset - 1]]
        ff_slots += [shifted(block, "ctx", offset) for block in near_blocks[1:]]
    mlp_in = gather_rows(3, "mlp_gather", mlp_norm.astype(narrow))

    ff_width = group_count * ff_cols
    gate_weight = jnp.concatenate([block[:ff_cols] for block in ff_slots], axis=0)
    up_weight = jnp.concatenate([block[ff_cols : 2 * ff_cols] for block in ff_slots], axis=0)
    down_weight = jnp.concatenate([block[2 * ff_cols :] for block in ff_slots], axis=0)
    wide_ff = jax.ShapeDtypeStruct((query_rows, ff_width), jnp.float32)
    narrow_ff = jax.ShapeDtypeStruct((query_rows, ff_width), narrow)
    narrow_rows = jax.ShapeDtypeStruct((query_rows, model_width), narrow)
    gate_pre, up_pre, hidden, down_part = pl.pallas_call(
        mlp_forward_kernel,
        out_shape=[wide_ff, wide_ff, narrow_ff, narrow_rows],
        name="mlp_forward",
    )(mlp_in, gate_weight, up_weight, down_weight)
    (down_blocks,) = exchange(
        4,
        "down_scatter",
        [("scatter", ("head",), down_part.reshape(head_count, tok_rows, model_width))],
    )
    down_raw = add_up(down_blocks)
    down_normed, inverse_down = norm_rows(down_raw, norm_gains[3])
    block_out = (middle + down_normed).astype(narrow)
    cot_wide = cotangent.astype(jnp.float32)
    grad_down_raw, gain_three = norm_back(down_raw, inverse_down, norm_gains[3], cot_wide)
    grad_down_in = gather_rows(5, "grad_down_gather", grad_down_raw.astype(narrow))
    grad_gate_in, grad_up_in, grad_mlp_part = pl.pallas_call(
        mlp_backward_kernel,
        out_shape=[narrow_ff, narrow_ff, narrow_rows],
        name="mlp_backward",
    )(grad_down_in, gate_weight, up_weight, down_weight, gate_pre, up_pre)
    slots = (ctx_count, dp_count, ff_cols, model_width)
    ff_terms = jnp.concatenate(
        [
            rows_dot(grad_gate_in, mlp_in, 0, 0).astype(narrow).reshape(slots),
            rows_dot(grad_up_in, mlp_in, 0, 0).astype(narrow).reshape(slots),
            rows_dot(hidden, grad_down_in, 0, 0).astype(narrow).reshape(slots),
        ],
        axis=2,
    )
    half = dp_count // 2
    grad_mlp_blocks, ff_early = exchange(
        6,
        "grad_mlp_scatter",
        [
            (
                "scatter",
                ("head",),
                grad_mlp_part.reshape(head_count, tok_rows, model_width),
            ),
            ("relative", ("ctx",), ff_terms[:, :half]),
        ],
        (("head",), ("ctx",)),
    )
    grad_mlp_in = add_up(grad_mlp_blocks)
    grad_mid_part, gain_two = norm_back(middle, inverse_mid, norm_gains[2], grad_mlp_in)
    grad_middle = cot_wide + grad_mid_part
    grad_branch_raw, gain_one = norm_back(branch, inverse_branch, norm_gains[1], grad_middle)
    grad_branch_blocks, ff_late = exchange(
        7,
        "grad_branch_gather",
        [
            ("gather", ("head",), grad_branch_raw.astype(narrow)),
            ("relative", ("ctx",), ff_terms[:, half:]),
        ],
        (("head",), ("ctx",)),
    )
    grad_branch = grad_branch_blocks.reshape(query_rows, model_width)
    ff_sums = jnp.concatenate([add_up(ff_early), add_up(ff_late)], axis=0).astype(narrow)
    head_grad = rows_dot(grad_branch, out_weight, 1, 1).astype(narrow)
    row_delta = jnp.sum(head_grad.astype(jnp.float32) * attn_exact, axis=1, keepdims=True)
    grad_probs = rows_dot(head_grad, all_values, 1, 1)
    grad_scores = (probs_wide * (grad_probs - row_delta)).astype(narrow)
    value_sums = rows_dot(prob_rows, head_grad, 0, 0)
    key_sums = rows_dot(grad_scores, head_query, 0, 0)
    grad_rot_query = rows_dot(grad_scores, all_keys, 1, 0)
    query_back = rotate(grad_rot_query * score_scale, cosine_own, -sine_own)
    grad_query_raw, gain_query = norm_back(query_raw, inverse_query, qk_gains[0], query_back)
    key_back = rotate(key_sums, cosine, -sine_part)
    grad_key_raw, gain_key = norm_back(key_raw, inverse_key, qk_gains[1], key_back)
    grad_query_in = grad_query_raw.astype(narrow)
    grad_key_in = grad_key_raw.astype(narrow)
    grad_value_in = value_sums.astype(narrow)
    grad_attn_part = rows_dot(grad_key_in, key_weight, 1, 0) + rows_dot(
        grad_value_in, value_weight, 1, 0
    )
    own_part = lax.dynamic_slice_in_dim(grad_attn_part, first_query, query_rows) + rows_dot(
        grad_query_in, query_weight, 1, 0
    )
    grad_attn_part = lax.dynamic_update_slice_in_dim(grad_attn_part, own_part, first_query, 0)
    head_terms = jnp.concatenate(
        [
            rows_dot(grad_query_in, attn_in, 0, 0).reshape(group_count, query_cols, model_width),
            rows_dot(attn_out, grad_branch, 0, 0).reshape(group_count, query_cols, model_width),
        ],
        axis=1,
    ).astype(narrow)
    planes = (dp_count, every_count // dp_count, key_cols, model_width)
    key_value_terms = jnp.concatenate(
        [
            rows_dot(grad_key_in, attn_in_all, 0, 0).reshape(planes),
            rows_dot(grad_value_in, attn_in_all, 0, 0).reshape(planes),
        ],
        axis=2,
    ).astype(narrow).transpose(1, 0, 2, 3)
    head_terms = head_terms.reshape(dp_count, ctx_count, 2 * query_cols, model_width)
    grad_attn_blocks, head_blocks, key_value_blocks, ff_blocks = exchange(
        8,
        "last_scatter",
        [
            (
                "scatter",
                sequence_axes,
                grad_attn_part.astype(narrow).reshape(-1, tok_rows, model_width),
            ),
            ("scatter", ("ctx",), head_terms.transpose(1, 0, 2, 3)),
            ("scatter", sequence_axes, key_value_terms),
            ("relative", ("dp",), ff_sums),
        ],
        (sequence_axes, ("dp",)),
    )
    ff_own = add_up(ff_blocks)
    grad_attn_in = add_up(grad_attn_blocks)
    grad_in_part, gain_zero = norm_back(input_wide, inverse_in, norm_gains[0], grad_attn_in)
    d_block_in = (grad_middle + grad_in_part).astype(narrow)

    pad = ((0, 0), (0, model_width - head_width))
    gain_terms = jnp.concatenate(
        [
            jnp.sum(gain_zero, axis=0, keepdims=True),
            jnp.sum(gain_one, axis=0, keepdims=True),
            jnp.sum(gain_two, axis=0, keepdims=True),
            jnp.sum(gain_three, axis=0, keepdims=True),
            jnp.pad(jnp.sum(gain_query, axis=0, keepdims=True), pad),
            jnp.pad(jnp.sum(gain_key, axis=0, keepdims=True), pad),
            jnp.zeros((2, model_width), jnp.float32),
        ],
        axis=0,
    )
    gain_blocks, head_blocks, key_value_blocks = exchange(
        9,
        "depth_exchange",
        [
            ("gather", ("dp",), gain_terms),
            ("scatter", ("dp",), add_up(head_blocks).astype(narrow)),
            ("scatter", ("dp",), add_up(key_value_blocks).astype(narrow)),
        ],
    )
    head_own = lax.ppermute(add_up(head_blocks).astype(narrow), every_axis, to_owners).astype(
        jnp.float32
    )
    (gain_blocks,) = exchange(10, "gain_gather", [("gather", sequence_axes, add_up(gain_blocks))])
    gains = add_up(gain_blocks)
    key_value_own = add_up(key_value_blocks)
    return (
        block_out,
        d_block_in,
        gains[:4],
        gains[4:6, :head_width],
        head_own[:query_cols].T,
        key_value_own[:key_cols].T,
        key_value_own[key_cols:].T,
        head_own[query_cols:],
        ff_own[:ff_cols].T,
        ff_own[ff_cols : 2 * ff_cols].T,
        ff_own[2 * ff_cols :],
    )


def solution(mesh):
    in_specs = (
        P(("dp", "ctx", "head"), None),
        P(("dp", "ctx", "head"), None),
        P(("dp", "ctx")),
        P(),
        P(),
        P(None, ("dp", "ctx", "head")),
        P(None, ("dp", "ctx", "head")),
        P(None, ("dp", "ctx", "head")),
        P(("dp", "ctx", "head"), None),
        P(None, ("dp", "ctx", "head")),
        P(None, ("dp", "ctx", "head")),
        P(("dp", "ctx", "head"), None),
    )
    out_specs = (
        P(("dp", "ctx", "head"), None),
        P(("dp", "ctx", "head"), None),
        P(),
        P(),
        P(None, ("dp", "ctx", "head")),
        P(None, ("dp", "ctx", "head")),
        P(None, ("dp", "ctx", "head")),
        P(("dp", "ctx", "head"), None),
        P(None, ("dp", "ctx", "head")),
        P(None, ("dp", "ctx", "head")),
        P(("dp", "ctx", "head"), None),
    )
    return jax.shard_map(local, mesh=mesh, in_specs=in_specs, out_specs=out_specs, check_vma=False)
```
